256 devices in a mesh: ctx: 32 (over z, y_hi, core), head: 8 (over x, y_lo).
Axes of the slice: x: 4, y: 4 (y_hi: 2, y_lo: 2; y = y_hi * 2 + y_lo), z: 8, core: 2. Of those that a mesh axis runs over, the one named last changes fastest.
Arguments:
- queries: bfloat16 [4096, 64, 128], P('ctx', 'head'), may hold values from -200 to 200
- new_keys: bfloat16 [4096, 8, 128], P('ctx', 'head'), may hold values from -6 to 6
- new_values: bfloat16 [4096, 8, 128], P('ctx', 'head'), may hold values from -6 to 6
- pool_keys: bfloat16 [256, 32, 8, 128], P('ctx', None, 'head'), may hold values from -6 to 6
- pool_values: bfloat16 [256, 32, 8, 128], P('ctx', None, 'head'), may hold values from -6 to 6
- o_weight: bfloat16 [8192, 8192], P('head', 'ctx'), may hold values from -2 to 2
- page_list: int32 [64], replicated, may hold values from 0 to 255, as said below
Outputs:
- projected: bfloat16 [4096, 8192], P('ctx', 'head')
The draws below stay inside these ranges and needn't reach their ends.
Inputs may be any that keep to these rules, and one draw needn't show every extreme that they name: page_list names 64 distinct pool slots; slot p lies on cycle position p // 8; one cycle position holds exactly 4 of them and none holds more; some hold none.
All inputs are finite; a program needn't handle non-finite values.
Results may differ from the reference program's by a relative error of at most 0.015.
Values may be sent and summed in bfloat16 or wider, within the bound.
A program may use at most 192 MiB of HBM per device.

```python
import math
import jax
import jax.numpy as jnp
from jax import lax

D = 8192
QH = 64
KVH = 8
HD = 128
PAGE = 32
PG_DEV = 2
SLOTS = 8
OWNERS = 32
PAGES = 64
POOL = 256
PREFIX = 2048
SPAN = 4096


def drawn_pair(key):
    base = jax.random.fold_in(key, 11)
    first, second = jax.random.split(base, 2)
    queries = jnp.clip(jax.random.normal(first, (SPAN, QH, HD), jnp.float32), -5.0, 5.0)
    keys = jnp.clip(jax.random.normal(second, (SPAN, KVH, HD), jnp.float32), -5.0, 5.0)
    return (queries, keys)


def draw_queries(key, part):
    queries, keys = drawn_pair(key)
    return queries.astype(jnp.bfloat16)


def draw_new_keys(key, part):
    queries, keys = drawn_pair(key)
    return keys.astype(jnp.bfloat16)


def draw_page_list(key, part):
    first, second, third, fourth = jax.random.split(jax.random.fold_in(key, 23), 4)
    order = jax.random.permutation(first, OWNERS)
    moves = jax.random.randint(second, (OWNERS // 2,), 0, PG_DEV + 1)
    moves = moves.at[0].set(PG_DEV)
    pair_counts = jnp.stack([PG_DEV + moves, PG_DEV - moves], axis=1).reshape(OWNERS)
    counts = jnp.zeros((OWNERS,), jnp.int32).at[order].set(pair_counts.astype(jnp.int32))
    slot_score = jax.random.randint(third, (OWNERS, SLOTS), 0, 1024) * SLOTS + jnp.arange(SLOTS)[None, :]
    permuted = jnp.argsort(slot_score, axis=1)
    ranks = jnp.argsort(permuted, axis=1)
    live = ranks < counts[:, None]
    slot_ids = (jnp.arange(OWNERS)[:, None] * SLOTS + jnp.arange(SLOTS)[None, :]).reshape(POOL)
    shuffle = jax.random.randint(fourth, (POOL,), 0, 1024)
    ranking = (1 - live.reshape(POOL).astype(jnp.int32)) * (1 << 22) + shuffle * POOL + slot_ids
    picked = jnp.argsort(ranking)[:PAGES]
    return slot_ids[picked].astype(jnp.int32)


def spiked(array, key, source, target, shards_of, factor):
    def block_of(dim):
        return (jnp.arange(array.shape[dim]) // (array.shape[dim] // shards_of)).reshape((-1,) + (1,) * (array.ndim - 1 - dim))

    one_side = jax.random.permutation(key, shards_of)[block_of(target)]
    second = (block_of(target) + shards_of // 2) % shards_of
    return jnp.where((block_of(source) == one_side) | (block_of(source) == second), factor * array, array)


def steps_of(rng, dims, shards, least, high):
    def one(position, parts):
        heights = jax.random.uniform(jax.random.fold_in(jax.random.fold_in(rng, 6), position), (parts,), jnp.float32, least / len(shards), high / len(shards))
        return jnp.repeat(jnp.exp(heights), dims[position] // parts).reshape((-1,) + (1,) * (len(dims) - position - 1))

    factor_of = one(*shards[0])
    for cut in shards[1:]:
        factor_of = factor_of * one(*cut)
    return factor_of


def bell_draw(own_key, dims, deviation, bound, pieces=(), held_as=jnp.bfloat16):
    array = jax.random.normal(own_key, dims, jnp.float32) * deviation
    if len(pieces) > 0:
        array = steps_of(own_key, dims, pieces, -0.22, 0.18) * array
    return jnp.clip(array, min=-bound, max=bound).astype(held_as)


def noise_with(own_key, dims, deviation, limit, pieces, heavy, kind=jnp.bfloat16):
    drawn = deviation * jax.random.normal(own_key, dims, jnp.float32)
    if pieces:
        drawn = drawn * steps_of(own_key, dims, pieces, -0.22, 0.18)
    return jnp.clip(spiked(drawn, jax.random.fold_in(own_key, 3), *heavy), -limit, limit).astype(kind)


def setup_inputs(seed: int = 0) -> dict:
    key_list = jax.random.split(jax.random.key(seed), 8)
    return {
        "queries": draw_queries(jax.random.fold_in(key_list[7], 71), 0),
        "new_keys": draw_new_keys(jax.random.fold_in(key_list[7], 71), 0),
        "new_values": bell_draw(key_list[2], (SPAN, KVH, HD), 1.0, 6.0, ((0, 32), (1, 8))),
        "pool_keys": bell_draw(key_list[3], (POOL, PAGE, KVH, HD), 1.0, 6.0, ((0, 32), (2, 8))),
        "pool_values": bell_draw(key_list[4], (POOL, PAGE, KVH, HD), 1.0, 6.0, ((0, 32), (2, 8))),
        "o_weight": noise_with(key_list[5], (QH * HD, D), (QH * HD // 256) ** -0.5, 2.0, ((0, 8), (1, 32)), (0, 1, 32, 2.75)),
        "page_list": draw_page_list(jax.random.fold_in(key_list[7], 71), 0),
    }


NEG = -1e+30

def reference(queries, new_keys, new_values, pool_keys, pool_values, o_weight, page_list):
    group = QH // KVH
    scale = 1.0 / math.sqrt(HD)
    prefix_keys = jnp.take(pool_keys, page_list, axis=0).reshape(PREFIX, KVH, HD)
    prefix_values = jnp.take(pool_values, page_list, axis=0).reshape(PREFIX, KVH, HD)
    all_keys = jnp.concatenate([prefix_keys, new_keys], axis=0).astype(jnp.float32)
    all_values = jnp.concatenate([prefix_values, new_values], axis=0).astype(jnp.float32)
    block = math.gcd(256, SPAN)
    positions = jnp.arange(PREFIX + SPAN).astype(jnp.int32)

    def one_block(index):
        start = (index * block).astype(jnp.int32)
        query_block = lax.dynamic_slice_in_dim(queries, start, block, 0).astype(jnp.float32)
        query_block = query_block.reshape(block, KVH, group, HD)
        scores = jnp.einsum('rkgd,skd->kgrs', query_block, all_keys) * scale
        rows = PREFIX + start + jnp.arange(block).astype(jnp.int32)
        seen = positions[None, :] <= rows[:, None]
        scores = jnp.where(seen, scores, NEG)
        top = lax.optimization_barrier(jnp.max(scores, axis=-1, keepdims=True))
        weights = jnp.where(seen, jnp.exp(scores - top), 0.0)
        total = lax.optimization_barrier(jnp.sum(weights, axis=-1))
        rounded = lax.optimization_barrier(weights.astype(jnp.bfloat16)).astype(jnp.float32)
        mixed = jnp.einsum('kgrs,skd->kgrd', rounded, all_values) / total[..., None]
        return mixed.transpose(2, 0, 1, 3).reshape(block, QH * HD).astype(jnp.bfloat16)
    attended = lax.map(one_block, jnp.arange(SPAN // block).astype(jnp.int32)).reshape(SPAN, QH * HD)
    return jnp.dot(attended, o_weight, preferred_element_type=jnp.float32).astype(jnp.bfloat16)
```

```python
import functools

import jax
import jax.numpy as jnp
from jax import lax
from jax.experimental import pallas as pl
from jax.experimental.pallas import tpu as pltpu
from jax.sharding import PartitionSpec as P

MESH = pl.DeviceIdType.MESH
NEG = -1e30
BF16 = jnp.bfloat16
F32 = jnp.float32

Z = 8
HEADS = 8
ROWS = 128
GROUP = 8
HD = 128
PAGE = 32
NEWP = ROWS // PAGE
LIVE = 4
BLKP = NEWP + LIVE
PAGES = 64
PREFIX = PAGES * PAGE
CHUNK = 512
MQ = ROWS * GROUP
NPRE = PREFIX // CHUNK
KDIM = 1024
WC = 256
NCH = NPRE + Z


def rem8(a):
    return lax.rem(a + 2 * Z, Z)


def kernel(
    c_scale,
    idx_ref, sel_ref, q_ref, nk_ref, nv_ref, pk_ref, pv_ref, w_ref,
    out_ref,
    kv, kpre, vpre, s_ref, m_ref, acc, osc, apl, wg, pb, rsb, fs,
    ys, yr, zs, zr, cs, cr, ws, wr, asn, arc, rss, rsr, fss, fsr,
):
    ctx = lax.axis_index("ctx")
    head = lax.axis_index("head")
    z = ctx // 4
    yh = lax.rem(ctx // 2, 2)
    co = lax.rem(ctx, 2)
    pos = yh * 2 + co
    half = lax.rem(head, 2)
    fpos = head // 2

    core_dev = (z * 4 + yh * 2 + (1 - co), head)
    y_dev = (z * 4 + (1 - yh) * 2 + co, head)
    up_dev = (rem8(z + 1) * 4 + pos, head)
    dn_dev = (rem8(z - 1) * 4 + pos, head)

    def send(src, dst, ss, rs, dev):
        return pltpu.make_async_remote_copy(
            src_ref=src, dst_ref=dst, send_sem=ss, recv_sem=rs, device_id=dev, device_id_type=MESH
        )

    for i, (new_ref, pool_ref) in enumerate(((nk_ref, pk_ref), (nv_ref, pv_ref))):
        kv[i, z, yh, co, 0:NEWP] = new_ref[...]
        for j in range(LIVE):
            kv[i, z, yh, co, NEWP + j] = pool_ref[sel_ref[j]]

    bar = pltpu.get_barrier_semaphore()
    for dev in (core_dev, y_dev, up_dev, dn_dev):
        pl.semaphore_signal(bar, inc=1, device_id=dev, device_id_type=MESH)
    for j in range(1, HEADS):
        pl.semaphore_signal(bar, inc=1, device_id=(ctx, lax.rem(head + j, HEADS)), device_id_type=MESH)
    mine = (fpos == pos).astype(jnp.int32)
    for sp in range(4):
        for hf in range(2):
            skip = jnp.logical_and(sp == pos, 2 * pos + hf == head)

            @pl.when(jnp.logical_not(skip))
            def _():
                pl.semaphore_signal(
                    bar, inc=1, device_id=(z * 4 + sp, 2 * pos + hf), device_id_type=MESH
                )

    pl.semaphore_wait(bar, 4 + (HEADS - 1) + HEADS - mine)

    sends = []

    def go(cp):
        cp.start()
        sends.append(cp)

    def y_copy(i, blk):
        return send(kv.at[i, z, blk, co], kv.at[i, z, blk, co], ys.at[i], yr.at[i], y_dev)

    def core_pair(i, plane, n):
        ref = kv.at[i, plane, :, co]
        return send(ref, ref, cs.at[i, n], cr.at[i, n], core_dev)

    def core_one(i, plane, blk, n):
        ref = kv.at[i, plane, blk, co]
        return send(ref, ref, cs.at[i, n], cr.at[i, n], core_dev)

    def core_wait(i, plane, n):
        ref = kv.at[i, plane, :, 1 - co]
        send(ref, ref, cs.at[i, n], cr.at[i, n], core_dev).wait_recv()

    def core_wait_one(i, plane, blk, n):
        ref = kv.at[i, plane, blk, 1 - co]
        send(ref, ref, cs.at[i, n], cr.at[i, n], core_dev).wait_recv()

    def ring(i, d, plane, hop):
        ref = kv.at[i, plane, :, co]
        return send(ref, ref, zs.at[i, d, hop], zr.at[i, d, hop], up_dev if d == 0 else dn_dev)

    def ring_half(i, d, plane, hop):
        ref = kv.at[i, plane, d, co]
        return send(ref, ref, zs.at[i, d, hop], zr.at[i, d, hop], up_dev if d == 0 else dn_dev)

    def plane_at(d, k):
        return rem8(z - k) if d == 0 else rem8(z + k)

    for i in range(2):
        go(y_copy(i, yh))
    for i in range(2):
        y_copy(i, 1 - yh).wait_recv()
        for d in range(2):
            go(ring(i, d, z, 0))
        go(core_pair(i, z, 0))
    for k in range(1, 4):
        for i in range(2):
            for d in range(2):
                plane = plane_at(d, k)
                ring(i, d, plane, k - 1).wait_recv()
                if k < 3:
                    go(ring(i, d, plane, k))
                else:
                    go(ring_half(i, d, plane, k))
                go(core_pair(i, plane, 1 + 2 * (k - 1) + d))

    WH = KDIM // 2

    def w_own(d, hf):
        rows = pl.ds(hf * WH, WH)
        return send(
            w_ref.at[rows], wg.at[z, rows], ws.at[d, 0, hf], wr.at[d, 0, hf],
            up_dev if d == 0 else dn_dev,
        )

    def w_hop(d, k, hf):
        ref = wg.at[plane_at(d, k), pl.ds(hf * WH, WH)]
        return send(ref, ref, ws.at[d, k, hf], wr.at[d, k, hf], up_dev if d == 0 else dn_dev)

    def w_wait(d, k, hf):
        ref = wg.at[plane_at(d, k), pl.ds(hf * WH, WH)]
        send(
            ref, ref, ws.at[d, k - 1, hf], wr.at[d, k - 1, hf], up_dev if d == 0 else dn_dev
        ).wait_recv()

    for hf in range(2):
        for d in range(2):
            go(w_own(d, hf if d == 0 else 1 - hf))

    for i in range(2):
        for d in range(2):
            plane = plane_at(d, 4)
            ring_half(i, d, plane, 3).wait_recv()
            go(core_one(i, plane, d, 7 + d))
        core_wait(i, z, 0)
        for k in range(1, 4):
            for d in range(2):
                core_wait(i, plane_at(d, k), 1 + 2 * (k - 1) + d)
        for d in range(2):
            core_wait_one(i, plane_at(d, 4), d, 7 + d)

    def pump(k, t):
        for d in range(2):
            hf = t if d == 0 else 1 - t
            w_wait(d, k, hf)
            if k < 3 or t == 0:
                go(w_hop(d, k, hf))

    def compact(n, carry):
        blk = idx_ref[n] // BLKP
        pg = lax.rem(idx_ref[n], BLKP)
        bz, by, bc = blk // 4, lax.rem(blk // 2, 2), lax.rem(blk, 2)
        rows = pl.ds(pl.multiple_of(n * PAGE, PAGE), PAGE)
        kpre[rows, :] = kv[0, bz, by, bc, pg]
        vpre[rows, :] = kv[1, bz, by, bc, pg]
        return carry

    lax.fori_loop(0, PAGES, compact, 0)

    def scores(keys):
        return lax.dot_general(
            q_ref[...], keys, (((1,), (1,)), ((), ())), preferred_element_type=F32
        )

    def fold(s):
        top = s[:, 0:128]
        for n in range(1, CHUNK // 128):
            top = jnp.maximum(top, s[:, n * 128 : (n + 1) * 128])
        return top

    def plane_of(i, plane):
        return kv[i, plane, :, :, 0:NEWP].reshape(CHUNK, HD)

    own = scores(plane_of(0, z))
    row = lax.broadcasted_iota(jnp.int32, (MQ, CHUNK), 0) // GROUP + pos * ROWS
    col = lax.broadcasted_iota(jnp.int32, (MQ, CHUNK), 1)
    own = jnp.where(col <= row, own, NEG)
    s_ref[NPRE] = own
    m_ref[...] = fold(own)

    def first_pre(n, carry):
        s = scores(kpre[pl.ds(pl.multiple_of(n * CHUNK, CHUNK), CHUNK), :])
        s_ref[n] = s
        m_ref[...] = jnp.maximum(m_ref[...], fold(s))
        return carry

    def first_new(n, carry):
        s = scores(plane_of(0, n))
        s_ref[NPRE + 1 + n] = s
        m_ref[...] = jnp.maximum(m_ref[...], fold(s))
        return carry

    lax.fori_loop(0, NPRE, first_pre, 0)
    lax.fori_loop(0, z, first_new, 0)
    m_ref[...] = jnp.broadcast_to(jnp.max(m_ref[...], axis=1, keepdims=True), (MQ, 128))

    pump(1, 0)

    ones = jnp.ones((CHUNK, 128), BF16)

    def absorb(slot, values, fresh):
        top = m_ref[...]
        parts = []
        for n in range(CHUNK // 128):
            s = s_ref[slot, :, n * 128 : (n + 1) * 128]
            parts.append(jnp.exp2((s - top) * c_scale).astype(BF16))
        p = jnp.concatenate(parts, axis=1)
        o = jnp.dot(p, jnp.concatenate([values, ones], axis=1), preferred_element_type=F32)
        if fresh:
            acc[...] = o
        else:
            acc[...] += o

    absorb(NPRE, plane_of(1, z), True)

    def second_pre(n, carry):
        absorb(n, vpre[pl.ds(pl.multiple_of(n * CHUNK, CHUNK), CHUNK), :], False)
        return carry

    def second_new(n, carry):
        absorb(NPRE + 1 + n, plane_of(1, n), False)
        return carry

    lax.fori_loop(0, NPRE, second_pre, 0)
    pump(1, 1)
    lax.fori_loop(0, z, second_new, 0)

    osc[...] = acc[:, 0:128] / acc[:, 128:256]
    for g in range(GROUP):
        apl[pos, :, g * HD : (g + 1) * HD] = osc[pl.ds(g, ROWS, stride=GROUP), :].astype(BF16)

    def a_copy(blk, n, dev):
        return send(apl.at[blk], apl.at[blk], asn.at[n], arc.at[n], dev)

    other = (1 - yh) * 2 + co
    go(a_copy(pos, 0, y_dev))
    go(a_copy(pos, 1, core_dev))
    pump(2, 0)
    a_copy(other, 0, y_dev).wait_recv()
    go(a_copy(other, 2, core_dev))
    a_copy(yh * 2 + 1 - co, 1, core_dev).wait_recv()
    a_copy((1 - yh) * 2 + 1 - co, 2, core_dev).wait_recv()

    rows_a = apl[...].reshape(4 * ROWS, KDIM)
    order = [(0, 0)] + [(d, k) for k in range(1, 4) for d in range(2)] + [(0, 4)]

    def rs_copy(n, j):
        t = lax.rem(head + j, HEADS)
        return send(pb.at[n, t], rsb.at[n, head], rss.at[n, j], rsr.at[n, j], (ctx, t))

    def project(n):
        d, k = order[n]
        if k == 0:
            w = w_ref[...]
        else:
            w = wg[plane_at(d, k)]
        res = jnp.dot(rows_a, w, preferred_element_type=F32).astype(BF16)
        pb[n] = res.reshape(HEADS, 64, WC)
        for j in range(1, HEADS):
            go(rs_copy(n, j))

    def finish(n):
        d, k = order[n]
        total = pb[n, head].astype(F32)
        for j in range(1, HEADS):
            s = lax.rem(head - j + HEADS, HEADS)
            ref = rsb.at[n, s]
            send(ref, ref, rss.at[n, j], rsr.at[n, j], (ctx, s)).wait_recv()
            total = total + rsb[n, s].astype(F32)
        dest = plane_at(d, k)
        local = jnp.logical_and(fpos == pos, dest == head)
        rows = pl.ds(pl.multiple_of(half * 64, 64), 64)
        cols = pl.ds(pl.multiple_of(pos * WC, WC), WC)
        done = total.astype(BF16)
        fs[n] = done

        @pl.when(local)
        def _():
            out_ref[rows, cols] = done

        @pl.when(jnp.logical_not(local))
        def _():
            send(
                fs.at[n], out_ref.at[rows, cols], fss.at[n], fsr.at[pos, half], (z * 4 + fpos, dest)
            ).start()

    project(0)
    pump(2, 1)
    project(1)
    project(2)
    pump(3, 0)
    project(3)
    project(4)
    finish(0)
    pump(3, 1)
    finish(1)
    finish(2)
    project(5)
    project(6)
    finish(3)
    finish(4)
    w_wait(0, 4, 0)
    w_wait(1, 4, 1)
    project(7)
    finish(5)
    finish(6)
    finish(7)

    for sp in range(4):
        for hf in range(2):
            skip = jnp.logical_and(sp == pos, 2 * pos + hf == head)

            @pl.when(jnp.logical_not(skip))
            def _():
                ref = out_ref.at[pl.ds(hf * 64, 64), pl.ds(sp * WC, WC)]
                send(ref, ref, fss.at[0], fsr.at[sp, hf], (z * 4 + sp, 2 * pos + hf)).wait_recv()

    for n in range(8):
        d, k = order[n]
        local = jnp.logical_and(fpos == pos, plane_at(d, k) == head)

        @pl.when(jnp.logical_not(local))
        def _():
            send(fs.at[n], fs.at[n], fss.at[n], fsr.at[0, 0], core_dev).wait_send()

    for cp in sends:
        cp.wait_send()


def on_device(queries, new_keys, new_values, pool_keys, pool_values, o_weight, page_list):
    rows, qheads, width = queries.shape
    c_scale = 1.4426950408889634 / (width ** 0.5)
    slots = pool_keys.shape[0]
    ctx = lax.axis_index("ctx")
    owner = page_list // slots
    same = owner[:, None] == owner[None, :]
    rank = jnp.sum((same & (page_list[None, :] < page_list[:, None])).astype(jnp.int32), axis=1)
    idx = owner * BLKP + NEWP + rank
    want = jnp.arange(LIVE, dtype=jnp.int32)
    hit = (owner[None, :] == ctx) & (rank[None, :] == want[:, None])
    sel = jnp.sum(jnp.where(hit, page_list[None, :] - ctx * slots, 0), axis=1)

    vmem = pl.BlockSpec(memory_space=pltpu.VMEM)
    smem = pl.BlockSpec(memory_space=pltpu.SMEM)
    dma = pltpu.SemaphoreType.DMA
    return pl.pallas_call(
        functools.partial(kernel, c_scale),
        out_shape=jax.ShapeDtypeStruct((ROWS, KDIM), BF16),
        in_specs=[smem, smem] + [vmem] * 6,
        out_specs=vmem,
        scratch_shapes=[
            pltpu.VMEM((2, Z, 2, 2, BLKP, PAGE, HD), BF16),
            pltpu.VMEM((PREFIX, HD), BF16),
            pltpu.VMEM((PREFIX, HD), BF16),
            pltpu.VMEM((NCH, MQ, CHUNK), F32),
            pltpu.VMEM((MQ, 128), F32),
            pltpu.VMEM((MQ, 2 * HD), F32),
            pltpu.VMEM((MQ, HD), F32),
            pltpu.VMEM((4, ROWS, KDIM), BF16),
            pltpu.VMEM((Z, KDIM, WC), BF16),
            pltpu.VMEM((8, HEADS, 64, WC), BF16),
            pltpu.VMEM((8, HEADS, 64, WC), BF16),
            pltpu.VMEM((8, 64, WC), BF16),
            dma((2,)), dma((2,)),
            dma((2, 2, 4)), dma((2, 2, 4)),
            dma((2, 9)), dma((2, 9)),
            dma((2, 4, 2)), dma((2, 4, 2)),
            dma((3,)), dma((3,)),
            dma((8, HEADS)), dma((8, HEADS)),
            dma((8,)), dma((4, 2)),
        ],
        compiler_params=pltpu.CompilerParams(
            collective_id=0, has_side_effects=True, vmem_limit_bytes=60 * 2**20
        ),
        name="attention_projection",
    )(
        idx, sel,
        queries.reshape(rows * qheads, width),
        new_keys.reshape(NEWP, PAGE, width),
        new_values.reshape(NEWP, PAGE, width),
        pool_keys.reshape(slots, PAGE, width),
        pool_values.reshape(slots, PAGE, width),
        o_weight,
    )


def solution(mesh):
    in_specs = (
        P("ctx", "head", None),
        P("ctx", "head", None),
        P("ctx", "head", None),
        P("ctx", None, "head", None),
        P("ctx", None, "head", None),
        P("head", "ctx"),
        P(),
    )
    out_specs = P("ctx", "head")
    return jax.shard_map(
        on_device, mesh=mesh, in_specs=in_specs, out_specs=out_specs, check_vma=False
    )
```

```python
import functools

import jax
import jax.numpy as jnp
from jax import lax
from jax.experimental import pallas as pl
from jax.experimental.pallas import tpu as pltpu
from jax.sharding import PartitionSpec as P

MESH = pl.DeviceIdType.MESH
NEG = -1e30
BF16 = jnp.bfloat16
F32 = jnp.float32

Z = 8
ROWS = 128
GROUP = 8
HD = 128
PAGE = 32
NEWP = ROWS // PAGE
LIVE = 4
BLKP = NEWP + LIVE
PAGES = 64
PREFIX = PAGES * PAGE
CHUNK = 512
MQ = ROWS * GROUP
NPRE = PREFIX // CHUNK
KDIM = 1024
WC = 256
NCH = NPRE + Z


def rem8(a):
    return lax.rem(a + 2 * Z, Z)


def kernel(
    c_scale,
    idx_ref, sel_ref, q_ref, nk_ref, nv_ref, pk_ref, pv_ref, w_ref,
    out_ref,
    kb, vb, kpre, vpre, s_ref, m_ref, acc, osc, apl, wg, pb, rsb, fs,
    ys, yr, vys, vyr, zs, zr, cs, cr, cs2, cr2, ws, wr, wys, wyr, asn, arc, acs, acr, rss, rsr, fss, fsr,
):
    ctx = lax.axis_index("ctx")
    head = lax.axis_index("head")
    z = ctx // 4
    yh = lax.rem(ctx // 2, 2)
    co = lax.rem(ctx, 2)
    pos = yh * 2 + co
    x = head // 2
    yl = lax.rem(head, 2)

    core_dev = (z * 4 + yh * 2 + (1 - co), head)
    y_dev = (z * 4 + (1 - yh) * 2 + co, head)
    near_dev = (ctx, x * 2 + 1 - yl)
    next_dev = (z * 4 + (1 - yh) * 2 + co, x * 2 + 1 - yl)
    up_dev = (rem8(z + 1) * 4 + pos, head)
    dn_dev = (rem8(z - 1) * 4 + pos, head)

    def send(src, dst, ss, rs, dev):
        return pltpu.make_async_remote_copy(
            src_ref=src, dst_ref=dst, send_sem=ss, recv_sem=rs, device_id=dev, device_id_type=MESH
        )

    for buf, new_ref, pool_ref in ((kb, nk_ref, pk_ref), (vb, nv_ref, pv_ref)):
        buf[z, yh, co, 0:NEWP] = new_ref[...]
        for j in range(LIVE):
            buf[z, yh, co, NEWP + j] = pool_ref[sel_ref[j]]

    WCOL = WC // 2
    my_cols = pl.ds(pl.multiple_of(yl * WCOL, WCOL), WCOL)
    wg[z, yl] = w_ref[:, my_cols]

    bar = pltpu.get_barrier_semaphore()
    for dev in (core_dev, y_dev, near_dev, next_dev, up_dev, dn_dev):
        pl.semaphore_signal(bar, inc=1, device_id=dev, device_id_type=MESH)
    for j in range(1, 4):
        pl.semaphore_signal(
            bar, inc=1, device_id=(ctx, lax.rem(x + j, 4) * 2 + yl), device_id_type=MESH
        )
    mine = (x == pos).astype(jnp.int32)
    for sp in range(4):
        for hf in range(2):
            skip = jnp.logical_and(sp == pos, pos * 2 + hf == head)

            @pl.when(jnp.logical_not(skip))
            def _():
                pl.semaphore_signal(
                    bar, inc=1, device_id=(z * 4 + sp, pos * 2 + hf), device_id_type=MESH
                )

    pl.semaphore_wait(bar, 9 + 8 - mine)

    sends = []

    def go(cp):
        cp.start()
        sends.append(cp)

    def plane_at(d, k):
        return rem8(z - k) if d == 0 else rem8(z + k)

    def zdev(d):
        return up_dev if d == 0 else dn_dev

    def y_copy(blk):
        ref = kb.at[z, blk, co]
        return send(ref, ref, ys.at[0], yr.at[0], y_dev)

    def k_ring(d, plane, hop):
        ref = kb.at[plane, :, co] if hop < 3 else kb.at[plane, d, co]
        return send(ref, ref, zs.at[0, d, hop], zr.at[0, d, hop], zdev(d))

    def k_core(plane, n, d, c):
        ref = kb.at[plane, :, c] if n < 7 else kb.at[plane, d, c]
        return send(ref, ref, cs.at[0, n], cr.at[0, n], core_dev)

    def v_part(plane, by, c, n, d):
        return vb.at[plane, by, c] if n < 7 else vb.at[plane, by, c, pl.ds(d * LIVE, LIVE)]

    def v_ring(d, plane, hop):
        ref = v_part(plane, yh, co, 7 if hop == 3 else 0, d)
        return send(ref, ref, zs.at[1, d, hop], zr.at[1, d, hop], zdev(d))

    def v_y(plane, n, d, by):
        ref = v_part(plane, by, co, n, d)
        return send(ref, ref, vys.at[n], vyr.at[n], y_dev)

    def v_core(plane, n, d, c):
        ref = v_part(plane, yh, c, n, d)
        return send(ref, ref, cs.at[1, n], cr.at[1, n], core_dev)

    def v_core2(plane, n, d, c):
        ref = v_part(plane, 1 - yh, c, n, d)
        return send(ref, ref, cs2.at[n], cr2.at[n], core_dev)

    WH = KDIM // 2

    def w_part(d, k, i):
        qt = i if d == 0 else i + 1 - 2 * (i % 2)
        side = yl if qt < 2 else 1 - yl
        return qt, wg.at[plane_at(d, k), side, pl.ds((qt % 2) * WH, WH)]

    def w_send(d, k, i):
        qt, ref = w_part(d, k, i)
        return send(ref, ref, ws.at[d, k, qt], wr.at[d, k, qt], zdev(d))

    def w_swap(hf, side):
        rows = pl.ds(hf * WH, WH)
        cols = pl.ds(pl.multiple_of((1 - yl) * WCOL, WCOL), WCOL)
        return send(w_ref.at[rows, cols], wg.at[z, side, rows], wys.at[hf], wyr.at[hf], near_dev)

    def w_own(i):
        for d in range(2):
            if i == 2:
                qt, ref = w_part(d, 0, i)
                w_swap(qt % 2, 1 - yl).wait_recv()
            go(w_send(d, 0, i))

    def pump(k, i):
        for d in range(2):
            qt, ref = w_part(d, k, i)
            send(ref, ref, ws.at[d, k - 1, qt], wr.at[d, k - 1, qt], zdev(d)).wait_recv()
            if k < 3 or (k == 3 and i % 2 == 0):
                go(w_send(d, k, i))

    steps = [(0, 0, 0)] + [(1 + 2 * (k - 1) + d, d, k) for k in range(1, 4) for d in range(2)]
    steps += [(7, 0, 4), (8, 1, 4)]

    go(y_copy(yh))
    for d in range(2):
        go(v_ring(d, z, 0))
    go(v_y(z, 0, 0, yh))
    for hf in range(2):
        go(w_swap(hf, yl))
    go(v_core(z, 0, 0, co))
    w_own(0)
    y_copy(1 - yh).wait_recv()
    for d in range(2):
        go(k_ring(d, z, 0))
    go(k_core(z, 0, 0, co))
    w_own(1)
    for k in range(1, 4):
        for d in range(2):
            n = 1 + 2 * (k - 1) + d
            plane = plane_at(d, k)
            v_ring(d, plane, k - 1).wait_recv()
            go(v_ring(d, plane, k))
            go(v_y(plane, n, d, yh))
            go(v_core(plane, n, d, co))
        for d in range(2):
            n = 1 + 2 * (k - 1) + d
            plane = plane_at(d, k)
            k_ring(d, plane, k - 1).wait_recv()
            go(k_ring(d, plane, k))
            go(k_core(plane, n, d, co))
        if k < 3:
            w_own(k + 1)

    def compact(src, dst):
        def one(n, carry):
            blk = idx_ref[n] // BLKP
            pg = lax.rem(idx_ref[n], BLKP)
            bz, by, bc = blk // 4, lax.rem(blk // 2, 2), lax.rem(blk, 2)
            dst[pl.ds(pl.multiple_of(n * PAGE, PAGE), PAGE), :] = src[bz, by, bc, pg]
            return carry

        lax.fori_loop(0, PAGES, one, 0)

    def scores(keys):
        return lax.dot_general(
            q_ref[...], keys, (((1,), (1,)), ((), ())), preferred_element_type=F32
        )

    def fold(s):
        top = s[:, 0:128]
        for n in range(1, CHUNK // 128):
            top = jnp.maximum(top, s[:, n * 128 : (n + 1) * 128])
        return top

    def plane_of(buf, plane):
        return buf[plane, :, :, 0:NEWP].reshape(CHUNK, HD)

    def first(slot, keys):
        s = scores(keys)
        s_ref[slot] = s
        m_ref[...] = jnp.maximum(m_ref[...], fold(s))

    def first_pre(n, carry):
        first(n, kpre[pl.ds(pl.multiple_of(n * CHUNK, CHUNK), CHUNK), :])
        return carry

    def first_new(n, carry):
        first(NPRE + 1 + n, plane_of(kb, n))
        return carry

    def spread():
        return jnp.broadcast_to(jnp.max(m_ref[...], axis=1, keepdims=True), (MQ, 128))

    ones = jnp.ones((CHUNK, 128), BF16)

    def absorb(slot, values, fresh):
        top = m_ref[...]
        parts = []
        for n in range(CHUNK // 128):
            s = s_ref[slot, :, n * 128 : (n + 1) * 128]
            parts.append(jnp.exp2((s - top) * c_scale).astype(BF16))
        p = jnp.concatenate(parts, axis=1)
        o = jnp.dot(p, jnp.concatenate([values, ones], axis=1), preferred_element_type=F32)
        if fresh:
            acc[...] = o
        else:
            acc[...] += o

    def second_pre(n, carry):
        absorb(n, vpre[pl.ds(pl.multiple_of(n * CHUNK, CHUNK), CHUNK), :], False)
        return carry

    def second_new(n, carry):
        absorb(NPRE + 1 + n, plane_of(vb, n), False)
        return carry

    far = jnp.maximum(z - 4, 0)
    near = jnp.where(z >= 4, z - 3, 0)

    for i in range(3):
        pump(1, i)
    for n, d, k in steps[:7]:
        k_core(plane_at(d, k), n, d, 1 - co).wait_recv()

    own = scores(plane_of(kb, z))
    row = lax.broadcasted_iota(jnp.int32, (MQ, CHUNK), 0) // GROUP + pos * ROWS
    col = lax.broadcasted_iota(jnp.int32, (MQ, CHUNK), 1)
    own = jnp.where(col <= row, own, NEG)
    s_ref[NPRE] = own
    m_ref[...] = fold(own)
    lax.fori_loop(0, far, first_new, 0)
    lax.fori_loop(near, z, first_new, 0)
    m_ref[...] = spread()

    for n, d, k in steps[:7]:
        plane = plane_at(d, k)
        v_y(plane, n, d, 1 - yh).wait_recv()
        go(v_core2(plane, n, d, co))
    for d in range(2):
        plane = plane_at(d, 4)
        v_ring(d, plane, 3).wait_recv()
        go(v_y(plane, 7 + d, d, yh))
        go(v_core(plane, 7 + d, d, co))
    for d in range(2):
        plane = plane_at(d, 4)
        k_ring(d, plane, 3).wait_recv()
        go(k_core(plane, 7 + d, d, co))
    pump(1, 3)
    for n, d, k in steps[:7]:
        plane = plane_at(d, k)
        v_core(plane, n, d, 1 - co).wait_recv()
        v_core2(plane, n, d, 1 - co).wait_recv()

    absorb(NPRE, plane_of(vb, z), True)
    lax.fori_loop(0, far, second_new, 0)
    lax.fori_loop(near, z, second_new, 0)

    for n, d, k in steps[7:]:
        plane = plane_at(d, k)
        v_y(plane, n, d, 1 - yh).wait_recv()
        go(v_core2(plane, n, d, co))
        k_core(plane, n, d, 1 - co).wait_recv()
    pump(2, 0)
    compact(kb, kpre)
    osc[...] = m_ref[...]
    lax.fori_loop(0, NPRE, first_pre, 0)
    lax.fori_loop(far, near, first_new, 0)
    m_ref[...] = spread()
    for n, d, k in steps[7:]:
        plane = plane_at(d, k)
        v_core(plane, n, d, 1 - co).wait_recv()
        v_core2(plane, n, d, 1 - co).wait_recv()
    pump(2, 1)
    compact(vb, vpre)
    keep = jnp.exp2((osc[...] - m_ref[...]) * c_scale)
    acc[:, 0:128] = acc[:, 0:128] * keep
    acc[:, 128:256] = acc[:, 128:256] * keep
    lax.fori_loop(0, NPRE, second_pre, 0)
    lax.fori_loop(far, near, second_new, 0)

    osc[...] = acc[:, 0:128] / acc[:, 128:256]
    for g in range(GROUP):
        apl[yl, yh, co, :, g * HD : (g + 1) * HD] = osc[pl.ds(g, ROWS, stride=GROUP), :].astype(BF16)

    blocks = ((yl, yh), (1 - yl, yh), (1 - yl, 1 - yh), (yl, 1 - yh))

    def a_ref(b, c, hf):
        return apl.at[blocks[b][0], blocks[b][1], c, pl.ds(hf * 64, 64)]

    def a_out(b, to, hf, dev):
        ref = a_ref(b, co, hf)
        return send(ref, ref, asn.at[to, hf], arc.at[to, hf], dev)

    def a_in(b, to, hf):
        ref = a_ref(b, co, hf)
        send(ref, ref, asn.at[to, hf], arc.at[to, hf], near_dev).wait_recv()

    def a_core(b, hf, c):
        ref = a_ref(b, c, hf)
        return send(ref, ref, acs.at[b, hf], acr.at[b, hf], core_dev)

    for i in range(2):
        go(a_out(0, 0, i, near_dev))
        go(a_out(0, 1, 1 - i, next_dev))
    for hf in range(2):
        go(a_core(0, hf, co))
    pump(2, 2)
    a_in(1, 0, 0)
    go(a_out(1, 2, 0, next_dev))
    a_in(2, 1, 1)
    go(a_out(2, 2, 1, near_dev))
    go(a_core(1, 0, co))
    go(a_core(2, 1, co))
    pump(2, 3)
    a_in(1, 0, 1)
    go(a_core(1, 1, co))
    a_in(2, 1, 0)
    go(a_core(2, 0, co))
    pump(3, 0)
    for hf in range(2):
        a_in(3, 2, hf)
        go(a_core(3, hf, co))
    for b in range(4):
        for hf in range(2):
            a_core(b, hf, 1 - co).wait_recv()

    order = [(0, 0)] + [(d, k) for k in range(1, 4) for d in range(2)] + [(0, 4)]

    def rs_copy(n, j):
        xt = lax.rem(x + j, 4)
        return send(
            pb.at[n, xt], rsb.at[n, x], rss.at[n, j], rsr.at[n, j], (ctx, xt * 2 + yl)
        )

    def project(*ns):
        res = None
        for side in range(2):
            w = [wg[plane_at(*order[n]), side] for n in ns]
            w = w[0] if len(w) == 1 else jnp.concatenate(w, axis=1)
            part = jnp.dot(
                apl[side].reshape(4 * ROWS, KDIM), w, preferred_element_type=F32
            )
            res = part if res is None else res + part
        res = res.astype(BF16)
        for i, n in enumerate(ns):
            pb[n] = res[:, i * WCOL : (i + 1) * WCOL].reshape(4, ROWS, WCOL)
        for n in ns:
            for j in (2, 1, 3):
                go(rs_copy(n, j))

    def finish(n):
        total = pb[n, x].astype(F32)
        for j in range(1, 4):
            s = lax.rem(x - j + 4, 4)
            ref = rsb.at[n, s]
            send(ref, ref, rss.at[n, j], rsr.at[n, j], (ctx, s * 2 + yl)).wait_recv()
            total = total + rsb[n, s].astype(F32)
        dest = plane_at(*order[n])
        local = jnp.logical_and(x == pos, dest == head)
        cols = pl.ds(pl.multiple_of(pos * WC + yl * WCOL, WCOL), WCOL)
        done = total.astype(BF16)
        fs[n] = done

        @pl.when(local)
        def _():
            out_ref[:, cols] = done

        @pl.when(jnp.logical_not(local))
        def _():
            send(
                fs.at[n], out_ref.at[:, cols], fss.at[n], fsr.at[pos, yl], (z * 4 + x, dest)
            ).start()

    project(0)
    project(1, 2)
    pump(3, 1)
    project(3, 4)
    finish(0)
    pump(3, 2)
    finish(1)
    pump(3, 3)
    project(5, 6)
    finish(2)
    finish(3)
    finish(4)
    for i in (0, 2):
        pump(4, i)
    project(7)
    finish(5)
    finish(6)
    finish(7)

    for sp in range(4):
        for hf in range(2):
            skip = jnp.logical_and(sp == pos, pos * 2 + hf == head)

            @pl.when(jnp.logical_not(skip))
            def _():
                ref = out_ref.at[:, pl.ds(sp * WC + hf * WCOL, WCOL)]
                send(ref, ref, fss.at[0], fsr.at[sp, hf], (z * 4 + sp, pos * 2 + hf)).wait_recv()

    for n in range(8):
        local = jnp.logical_and(x == pos, plane_at(*order[n]) == head)

        @pl.when(jnp.logical_not(local))
        def _():
            send(fs.at[n], fs.at[n], fss.at[n], fsr.at[0, 0], core_dev).wait_send()

    for cp in sends:
        cp.wait_send()


def on_device(queries, new_keys, new_values, pool_keys, pool_values, o_weight, page_list):
    rows, qheads, width = queries.shape
    c_scale = 1.4426950408889634 / (width ** 0.5)
    slots = pool_keys.shape[0]
    ctx = lax.axis_index("ctx")
    owner = page_list // slots
    same = owner[:, None] == owner[None, :]
    rank = jnp.sum((same & (page_list[None, :] < page_list[:, None])).astype(jnp.int32), axis=1)
    idx = owner * BLKP + NEWP + rank
    want = jnp.arange(LIVE, dtype=jnp.int32)
    hit = (owner[None, :] == ctx) & (rank[None, :] == want[:, None])
    sel = jnp.sum(jnp.where(hit, page_list[None, :] - ctx * slots, 0), axis=1)

    vmem = pl.BlockSpec(memory_space=pltpu.VMEM)
    smem = pl.BlockSpec(memory_space=pltpu.SMEM)
    dma = pltpu.SemaphoreType.DMA
    return pl.pallas_call(
        functools.partial(kernel, c_scale),
        out_shape=jax.ShapeDtypeStruct((ROWS, KDIM), BF16),
        in_specs=[smem, smem] + [vmem] * 6,
        out_specs=vmem,
        scratch_shapes=[
            pltpu.VMEM((Z, 2, 2, BLKP, PAGE, HD), BF16),
            pltpu.VMEM((Z, 2, 2, BLKP, PAGE, HD), BF16),
            pltpu.VMEM((PREFIX, HD), BF16),
            pltpu.VMEM((PREFIX, HD), BF16),
            pltpu.VMEM((NCH, MQ, CHUNK), F32),
            pltpu.VMEM((MQ, 128), F32),
            pltpu.VMEM((MQ, 2 * HD), F32),
            pltpu.VMEM((MQ, HD), F32),
            pltpu.VMEM((2, 2, 2, ROWS, KDIM), BF16),
            pltpu.VMEM((Z, 2, KDIM, WC // 2), BF16),
            pltpu.VMEM((8, 4, ROWS, WC // 2), BF16),
            pltpu.VMEM((8, 4, ROWS, WC // 2), BF16),
            pltpu.VMEM((8, ROWS, WC // 2), BF16),
            dma((1,)), dma((1,)), dma((9,)), dma((9,)),
            dma((2, 2, 4)), dma((2, 2, 4)),
            dma((2, 9)), dma((2, 9)), dma((9,)), dma((9,)),
            dma((2, 4, 4)), dma((2, 4, 4)), dma((2,)), dma((2,)),
            dma((3, 2)), dma((3, 2)), dma((4, 2)), dma((4, 2)),
            dma((8, 4)), dma((8, 4)),
            dma((8,)), dma((4, 2)),
        ],
        compiler_params=pltpu.CompilerParams(
            collective_id=0, has_side_effects=True, vmem_limit_bytes=60 * 2**20
        ),
        name="attention_projection",
    )(
        idx, sel,
        queries.reshape(rows * qheads, width),
        new_keys.reshape(NEWP, PAGE, width),
        new_values.reshape(NEWP, PAGE, width),
        pool_keys.reshape(slots, PAGE, width),
        pool_values.reshape(slots, PAGE, width),
        o_weight,
    )


def solution(mesh):
    in_specs = (
        P("ctx", "head", None),
        P("ctx", "head", None),
        P("ctx", "head", None),
        P("ctx", None, "head", None),
        P("ctx", None, "head", None),
        P("head", "ctx"),
        P(),
    )
    out_specs = P("ctx", "head")
    return jax.shard_map(
        on_device, mesh=mesh, in_specs=in_specs, out_specs=out_specs, check_vma=False
    )
```

```python
import functools

import jax
import jax.numpy as jnp
from jax import lax
from jax.experimental import pallas as pl
from jax.experimental.pallas import tpu as pltpu
from jax.sharding import PartitionSpec as P

MESH = pl.DeviceIdType.MESH
NEG = -1e30
BF16 = jnp.bfloat16
F32 = jnp.float32

Z = 8
ROWS = 128
GROUP = 8
HD = 128
PAGE = 32
NEWP = ROWS // PAGE
LIVE = 4
BLKP = NEWP + LIVE
PAGES = 64
PREFIX = PAGES * PAGE
CHUNK = 512
MQ = ROWS * GROUP
NPRE = PREFIX // CHUNK
KDIM = 1024
WC = 256
NCH = NPRE + Z


def rem8(a):
    return lax.rem(a + 2 * Z, Z)


def kernel(
    c_scale,
    idx_ref, sel_ref, q_ref, nk_ref, nv_ref, pk_ref, pv_ref, w_ref,
    out_ref,
    kb, vb, kpre, vpre, s_ref, m_ref, acc, osc, apl, wg, pb, rsb, fs,
    ys, yr, vys, vyr, zs, zr, cs, cr, cs2, cr2, ws, wr, wys, wyr, asn, arc, acs, acr, rss, rsr, fss, fsr,
):
    ctx = lax.axis_index("ctx")
    head = lax.axis_index("head")
    z = ctx // 4
    yh = lax.rem(ctx // 2, 2)
    co = lax.rem(ctx, 2)
    pos = yh * 2 + co
    x = head // 2
    yl = lax.rem(head, 2)
    cx, hx = x // 2, lax.rem(x, 2)

    core_dev = (z * 4 + yh * 2 + (1 - co), head)
    y_dev = (z * 4 + (1 - yh) * 2 + co, head)
    near_dev = (ctx, x * 2 + 1 - yl)
    next_dev = (z * 4 + (1 - yh) * 2 + co, x * 2 + 1 - yl)
    up_dev = (rem8(z + 1) * 4 + pos, head)
    dn_dev = (rem8(z - 1) * 4 + pos, head)

    def send(src, dst, ss, rs, dev):
        return pltpu.make_async_remote_copy(
            src_ref=src, dst_ref=dst, send_sem=ss, recv_sem=rs, device_id=dev, device_id_type=MESH
        )

    for buf, new_ref, pool_ref in ((kb, nk_ref, pk_ref), (vb, nv_ref, pv_ref)):
        buf[z, yh, co, 0:NEWP] = new_ref[...]
        for j in range(LIVE):
            buf[z, yh, co, NEWP + j] = pool_ref[sel_ref[j]]

    WCOL = WC // 2
    my_cols = pl.ds(pl.multiple_of(yl * WCOL, WCOL), WCOL)
    wg[z, yl] = w_ref[:, my_cols]

    bar = pltpu.get_barrier_semaphore()
    for dev in (core_dev, y_dev, near_dev, next_dev, up_dev, dn_dev):
        pl.semaphore_signal(bar, inc=1, device_id=dev, device_id_type=MESH)
    for j in range(1, 4):
        pl.semaphore_signal(
            bar, inc=1, device_id=(ctx, lax.rem(x + j, 4) * 2 + yl), device_id_type=MESH
        )
    mine = (cx == co).astype(jnp.int32)
    finals = [(sp, hf, side) for sp in range(4) for hf in range(2) for side in range(2)]

    def final_from(sp, hf, side):
        from_head = (2 * co + hf) * 2 + side
        return jnp.logical_and(sp == pos, from_head == head), (z * 4 + sp, from_head)

    for one in finals:
        skip, dev = final_from(*one)

        @pl.when(jnp.logical_not(skip))
        def _():
            pl.semaphore_signal(bar, inc=1, device_id=dev, device_id_type=MESH)

    pl.semaphore_wait(bar, 9 + 16 - mine)

    sends = []

    def go(cp):
        cp.start()
        sends.append(cp)

    def plane_at(d, k):
        return rem8(z - k) if d == 0 else rem8(z + k)

    def zdev(d):
        return up_dev if d == 0 else dn_dev

    def y_copy(blk):
        ref = kb.at[z, blk, co]
        return send(ref, ref, ys.at[0], yr.at[0], y_dev)

    def k_ring(d, plane, hop):
        ref = kb.at[plane, :, co] if hop < 3 else kb.at[plane, d, co]
        return send(ref, ref, zs.at[0, d, hop], zr.at[0, d, hop], zdev(d))

    def k_core(plane, n, d, c):
        ref = kb.at[plane, :, c] if n < 7 else kb.at[plane, d, c]
        return send(ref, ref, cs.at[0, n], cr.at[0, n], core_dev)

    def v_part(plane, by, c, n, d):
        return vb.at[plane, by, c] if n < 7 else vb.at[plane, by, c, pl.ds(d * LIVE, LIVE)]

    def v_ring(d, plane, hop):
        ref = v_part(plane, yh, co, 7 if hop == 3 else 0, d)
        return send(ref, ref, zs.at[1, d, hop], zr.at[1, d, hop], zdev(d))

    def v_y(plane, n, d, by):
        ref = v_part(plane, by, co, n, d)
        return send(ref, ref, vys.at[n], vyr.at[n], y_dev)

    def v_core(plane, n, d, c):
        ref = v_part(plane, yh, c, n, d)
        return send(ref, ref, cs.at[1, n], cr.at[1, n], core_dev)

    def v_core2(plane, n, d, c):
        ref = v_part(plane, 1 - yh, c, n, d)
        return send(ref, ref, cs2.at[n], cr2.at[n], core_dev)

    WH = KDIM // 2

    def w_part(d, k, i):
        qt = i if d == 0 else i + 1 - 2 * (i % 2)
        side = yl if qt < 2 else 1 - yl
        return qt, wg.at[plane_at(d, k), side, pl.ds((qt % 2) * WH, WH)]

    def w_send(d, k, i):
        qt, ref = w_part(d, k, i)
        return send(ref, ref, ws.at[d, k, qt], wr.at[d, k, qt], zdev(d))

    def w_swap(hf, side):
        rows = pl.ds(hf * WH, WH)
        cols = pl.ds(pl.multiple_of((1 - yl) * WCOL, WCOL), WCOL)
        return send(w_ref.at[rows, cols], wg.at[z, side, rows], wys.at[hf], wyr.at[hf], near_dev)

    def w_own(i):
        for d in range(2):
            if i == 2:
                qt, ref = w_part(d, 0, i)
                w_swap(qt % 2, 1 - yl).wait_recv()
            go(w_send(d, 0, i))

    def pump(k, i):
        for d in range(2):
            qt, ref = w_part(d, k, i)
            send(ref, ref, ws.at[d, k - 1, qt], wr.at[d, k - 1, qt], zdev(d)).wait_recv()
            if k < 3 or (k == 3 and i % 2 == 0):
                go(w_send(d, k, i))

    steps = [(0, 0, 0)] + [(1 + 2 * (k - 1) + d, d, k) for k in range(1, 4) for d in range(2)]
    steps += [(7, 0, 4), (8, 1, 4)]

    go(y_copy(yh))
    for d in range(2):
        go(v_ring(d, z, 0))
    go(v_y(z, 0, 0, yh))
    for hf in range(2):
        go(w_swap(hf, yl))
    go(v_core(z, 0, 0, co))
    w_own(0)
    y_copy(1 - yh).wait_recv()
    for d in range(2):
        go(k_ring(d, z, 0))
    go(k_core(z, 0, 0, co))
    w_own(1)
    for k in range(1, 4):
        for d in range(2):
            n = 1 + 2 * (k - 1) + d
            plane = plane_at(d, k)
            v_ring(d, plane, k - 1).wait_recv()
            go(v_ring(d, plane, k))
            go(v_y(plane, n, d, yh))
            go(v_core(plane, n, d, co))
        for d in range(2):
            n = 1 + 2 * (k - 1) + d
            plane = plane_at(d, k)
            k_ring(d, plane, k - 1).wait_recv()
            go(k_ring(d, plane, k))
            go(k_core(plane, n, d, co))
        if k < 3:
            w_own(k + 1)

    def compact(src, dst):
        def one(n, carry):
            blk = idx_ref[n] // BLKP
            pg = lax.rem(idx_ref[n], BLKP)
            bz, by, bc = blk // 4, lax.rem(blk // 2, 2), lax.rem(blk, 2)
            dst[pl.ds(pl.multiple_of(n * PAGE, PAGE), PAGE), :] = src[bz, by, bc, pg]
            return carry

        lax.fori_loop(0, PAGES, one, 0)

    def scores(keys):
        return lax.dot_general(
            q_ref[...], keys, (((1,), (1,)), ((), ())), preferred_element_type=F32
        )

    def fold(s):
        top = s[:, 0:128]
        for n in range(1, CHUNK // 128):
            top = jnp.maximum(top, s[:, n * 128 : (n + 1) * 128])
        return top

    def plane_of(buf, plane):
        return buf[plane, :, :, 0:NEWP].reshape(CHUNK, HD)

    def first(slot, keys):
        s = scores(keys)
        s_ref[slot] = s
        m_ref[...] = jnp.maximum(m_ref[...], fold(s))

    def first_pre(n, carry):
        first(n, kpre[pl.ds(pl.multiple_of(n * CHUNK, CHUNK), CHUNK), :])
        return carry

    def first_new(n, carry):
        first(NPRE + 1 + n, plane_of(kb, n))
        return carry

    def spread():
        return jnp.broadcast_to(jnp.max(m_ref[...], axis=1, keepdims=True), (MQ, 128))

    ones = jnp.ones((CHUNK, 128), BF16)

    def absorb(slot, values, rows, fresh):
        top = m_ref[rows, :]
        parts = []
        for n in range(CHUNK // 128):
            s = s_ref[slot, rows, n * 128 : (n + 1) * 128]
            parts.append(jnp.exp2((s - top) * c_scale).astype(BF16))
        p = jnp.concatenate(parts, axis=1)
        o = jnp.dot(p, jnp.concatenate([values, ones], axis=1), preferred_element_type=F32)
        if fresh:
            acc[rows, :] = o
        else:
            acc[rows, :] += o

    def second_pre(rows, n, carry):
        absorb(n, vpre[pl.ds(pl.multiple_of(n * CHUNK, CHUNK), CHUNK), :], rows, False)
        return carry

    def second_new(rows, n, carry):
        absorb(NPRE + 1 + n, plane_of(vb, n), rows, False)
        return carry

    every = pl.ds(0, MQ)

    far = jnp.maximum(z - 4, 0)
    near = jnp.where(z >= 4, z - 3, 0)

    for i in range(3):
        pump(1, i)
    for n, d, k in steps[:7]:
        k_core(plane_at(d, k), n, d, 1 - co).wait_recv()

    own = scores(plane_of(kb, z))
    row = lax.broadcasted_iota(jnp.int32, (MQ, CHUNK), 0) // GROUP + pos * ROWS
    col = lax.broadcasted_iota(jnp.int32, (MQ, CHUNK), 1)
    own = jnp.where(col <= row, own, NEG)
    s_ref[NPRE] = own
    m_ref[...] = fold(own)
    lax.fori_loop(0, far, first_new, 0)
    lax.fori_loop(near, z, first_new, 0)
    m_ref[...] = spread()

    for n, d, k in steps[:7]:
        plane = plane_at(d, k)
        v_y(plane, n, d, 1 - yh).wait_recv()
        go(v_core2(plane, n, d, co))
    for d in range(2):
        plane = plane_at(d, 4)
        v_ring(d, plane, 3).wait_recv()
        go(v_y(plane, 7 + d, d, yh))
        go(v_core(plane, 7 + d, d, co))
    for d in range(2):
        plane = plane_at(d, 4)
        k_ring(d, plane, 3).wait_recv()
        go(k_core(plane, 7 + d, d, co))
    pump(1, 3)
    for n, d, k in steps[:7]:
        plane = plane_at(d, k)
        v_core(plane, n, d, 1 - co).wait_recv()
        v_core2(plane, n, d, 1 - co).wait_recv()

    absorb(NPRE, plane_of(vb, z), every, True)
    lax.fori_loop(0, far, functools.partial(second_new, every), 0)
    lax.fori_loop(near, z, functools.partial(second_new, every), 0)

    for n, d, k in steps[7:]:
        plane = plane_at(d, k)
        v_y(plane, n, d, 1 - yh).wait_recv()
        go(v_core2(plane, n, d, co))
        k_core(plane, n, d, 1 - co).wait_recv()
    pump(2, 0)
    compact(kb, kpre)
    osc[...] = m_ref[...]
    lax.fori_loop(0, NPRE, first_pre, 0)
    lax.fori_loop(far, near, first_new, 0)
    m_ref[...] = spread()
    for n, d, k in steps[7:]:
        plane = plane_at(d, k)
        v_core(plane, n, d, 1 - co).wait_recv()
        v_core2(plane, n, d, 1 - co).wait_recv()
    compact(vb, vpre)

    blocks = ((yl, yh), (1 - yl, yh), (1 - yl, 1 - yh), (yl, 1 - yh))
    HR = ROWS // 2

    def a_ref(b, c, hf):
        return apl.at[blocks[b][0], blocks[b][1], c, pl.ds(hf * HR, HR)]

    def a_out(b, to, hf, dev):
        ref = a_ref(b, co, hf)
        return send(ref, ref, asn.at[to, hf], arc.at[to, hf], dev)

    def a_in(b, to, hf):
        ref = a_ref(b, co, hf)
        send(ref, ref, asn.at[to, hf], arc.at[to, hf], near_dev).wait_recv()

    def a_core(b, hf, c):
        ref = a_ref(b, c, hf)
        return send(ref, ref, acs.at[b, hf], acr.at[b, hf], core_dev)

    for hf in range(2):
        start = hf * (MQ // 2)
        rows = pl.ds(start, MQ // 2)
        keep = jnp.exp2((osc[rows, :] - m_ref[rows, :]) * c_scale)
        acc[rows, 0:128] = acc[rows, 0:128] * keep
        acc[rows, 128:256] = acc[rows, 128:256] * keep
        lax.fori_loop(0, NPRE, functools.partial(second_pre, rows), 0)
        lax.fori_loop(far, near, functools.partial(second_new, rows), 0)
        osc[rows, :] = acc[rows, 0:128] / acc[rows, 128:256]
        for g in range(GROUP):
            apl[yl, yh, co, hf * HR : (hf + 1) * HR, g * HD : (g + 1) * HD] = osc[
                pl.ds(start + g, HR, stride=GROUP), :
            ].astype(BF16)
        go(a_out(0, 0, hf, near_dev))
        go(a_out(0, 1, hf, next_dev))
        go(a_core(0, hf, co))
        pump(2, 1 + hf)

    order = [(0, 0)] + [(d, k) for k in range(1, 4) for d in range(2)] + [(0, 4)]

    def rs_copy(n, gi, j):
        xt = lax.rem(x + j, 4)
        g = yh if gi == 0 else 1 - yh
        return send(
            pb.at[n, g, xt], rsb.at[n, g, x], rss.at[n, gi, j], rsr.at[n, gi, j], (ctx, xt * 2 + yl)
        )

    def project(gi, *ns):
        g = yh if gi == 0 else 1 - yh
        res = None
        for side in range(2):
            w = [wg[plane_at(*order[n]), side] for n in ns]
            w = w[0] if len(w) == 1 else jnp.concatenate(w, axis=1)
            part = jnp.dot(
                apl[side, g].reshape(2 * ROWS, KDIM), w, preferred_element_type=F32
            )
            res = part if res is None else res + part
        res = res.astype(BF16)
        for i, n in enumerate(ns):
            pb[n, g] = res[:, i * WCOL : (i + 1) * WCOL].reshape(4, HR, WCOL)
        for n in ns:
            for j in (2, 1, 3):
                go(rs_copy(n, gi, j))

    def finish(n):
        dest = plane_at(*order[n])
        local = jnp.logical_and(cx == co, dest == head)
        rows = pl.ds(pl.multiple_of(hx * HR, HR), HR)
        cols = pl.ds(pl.multiple_of(pos * WC + yl * WCOL, WCOL), WCOL)
        for gi in range(2):
            g = yh if gi == 0 else 1 - yh
            total = pb[n, g, x].astype(F32)
            for j in range(1, 4):
                s = lax.rem(x - j + 4, 4)
                ref = rsb.at[n, g, s]
                send(ref, ref, rss.at[n, gi, j], rsr.at[n, gi, j], (ctx, s * 2 + yl)).wait_recv()
                total = total + rsb[n, g, s].astype(F32)
            done = total.astype(BF16)
            fs[n, gi] = done
            cp = send(
                fs.at[n, gi], out_ref.at[rows, cols], fss.at[n, gi], fsr.at[pos, hx, yl],
                (z * 4 + g * 2 + cx, dest),
            )
            if gi == 0:

                @pl.when(local)
                def _():
                    out_ref[rows, cols] = done

                @pl.when(jnp.logical_not(local))
                def _():
                    cp.start()
            else:
                go(cp)

    a_in(1, 0, 0)
    go(a_out(1, 2, 0, next_dev))
    go(a_core(1, 0, co))
    a_in(2, 1, 0)
    go(a_core(2, 0, co))
    a_in(1, 0, 1)
    go(a_core(1, 1, co))
    a_in(2, 1, 1)
    go(a_out(2, 2, 1, near_dev))
    go(a_core(2, 1, co))
    for b in range(2):
        for hf in range(2):
            a_core(b, hf, 1 - co).wait_recv()
    project(0, 0)
    project(0, 1, 2)
    a_in(3, 2, 0)
    go(a_core(3, 0, co))
    pump(2, 3)
    project(0, 3, 4)
    a_in(3, 2, 1)
    go(a_core(3, 1, co))
    pump(3, 0)
    for b in range(2, 4):
        for hf in range(2):
            a_core(b, hf, 1 - co).wait_recv()
    project(1, 0)
    project(1, 1, 2)
    pump(3, 1)
    pump(3, 2)
    project(1, 3, 4)
    finish(0)
    pump(3, 3)
    for gi in range(2):
        project(gi, 5, 6)
    finish(1)
    finish(2)
    pump(4, 0)
    finish(3)
    finish(4)
    pump(4, 2)
    for gi in range(2):
        project(gi, 7)
    finish(5)
    finish(6)
    finish(7)

    for sp, hf, side in finals:
        skip, dev = final_from(sp, hf, side)

        @pl.when(jnp.logical_not(skip))
        def _():
            ref = out_ref.at[pl.ds(hf * HR, HR), pl.ds(sp * WC + side * WCOL, WCOL)]
            send(ref, ref, fss.at[0, 0], fsr.at[sp, hf, side], dev).wait_recv()

    for n in range(8):
        local = jnp.logical_and(cx == co, plane_at(*order[n]) == head)

        @pl.when(jnp.logical_not(local))
        def _():
            send(fs.at[n, 0], fs.at[n, 0], fss.at[n, 0], fsr.at[0, 0, 0], core_dev).wait_send()

    for cp in sends:
        cp.wait_send()


def on_device(queries, new_keys, new_values, pool_keys, pool_values, o_weight, page_list):
    rows, qheads, width = queries.shape
    c_scale = 1.4426950408889634 / (width ** 0.5)
    slots = pool_keys.shape[0]
    owner = page_list // slots
    same = owner[:, None] == owner[None, :]
    rank = jnp.sum((same & (page_list[None, :] < page_list[:, None])).astype(jnp.int32), axis=1)
    idx = owner * BLKP + NEWP + rank
    ctx = lax.axis_index("ctx")
    want = jnp.arange(LIVE, dtype=jnp.int32)
    hit = (owner[None, :] == ctx) & (rank[None, :] == want[:, None])
    sel = jnp.sum(jnp.where(hit, page_list[None, :] - ctx * slots, 0), axis=1)

    vmem = pl.BlockSpec(memory_space=pltpu.VMEM)
    smem = pl.BlockSpec(memory_space=pltpu.SMEM)
    dma = pltpu.SemaphoreType.DMA
    return pl.pallas_call(
        functools.partial(kernel, c_scale),
        out_shape=jax.ShapeDtypeStruct((ROWS, KDIM), BF16),
        in_specs=[smem, smem] + [vmem] * 6,
        out_specs=vmem,
        scratch_shapes=[
            pltpu.VMEM((Z, 2, 2, BLKP, PAGE, HD), BF16),
            pltpu.VMEM((Z, 2, 2, BLKP, PAGE, HD), BF16),
            pltpu.VMEM((PREFIX, HD), BF16),
            pltpu.VMEM((PREFIX, HD), BF16),
            pltpu.VMEM((NCH, MQ, CHUNK), F32),
            pltpu.VMEM((MQ, 128), F32),
            pltpu.VMEM((MQ, 2 * HD), F32),
            pltpu.VMEM((MQ, HD), F32),
            pltpu.VMEM((2, 2, 2, ROWS, KDIM), BF16),
            pltpu.VMEM((Z, 2, KDIM, WC // 2), BF16),
            pltpu.VMEM((8, 2, 4, ROWS // 2, WC // 2), BF16),
            pltpu.VMEM((8, 2, 4, ROWS // 2, WC // 2), BF16),
            pltpu.VMEM((8, 2, ROWS // 2, WC // 2), BF16),
            dma((1,)), dma((1,)), dma((9,)), dma((9,)),
            dma((2, 2, 4)), dma((2, 2, 4)),
            dma((2, 9)), dma((2, 9)), dma((9,)), dma((9,)),
            dma((2, 4, 4)), dma((2, 4, 4)), dma((2,)), dma((2,)),
            dma((3, 2)), dma((3, 2)), dma((4, 2)), dma((4, 2)),
            dma((8, 2, 4)), dma((8, 2, 4)),
            dma((8, 2)), dma((4, 2, 2)),
        ],
        compiler_params=pltpu.CompilerParams(
            collective_id=0, has_side_effects=True, vmem_limit_bytes=60 * 2**20
        ),
        name="attention_projection",
    )(
        idx, sel,
        queries.reshape(rows * qheads, width),
        new_keys.reshape(NEWP, PAGE, width),
        new_values.reshape(NEWP, PAGE, width),
        pool_keys.reshape(slots, PAGE, width),
        pool_values.reshape(slots, PAGE, width),
        o_weight,
    )


def solution(mesh):
    in_specs = (
        P("ctx", "head", None),
        P("ctx", "head", None),
        P("ctx", "head", None),
        P("ctx", None, "head", None),
        P("ctx", None, "head", None),
        P("head", "ctx"),
        P(),
    )
    out_specs = P("ctx", "head")
    return jax.shard_map(
        on_device, mesh=mesh, in_specs=in_specs, out_specs=out_specs, check_vma=False
    )
```
